128 devices in a mesh: gx: 32 (over x, y_lo, z), gy: 4 (over y_hi, core).
Axes of the slice: x: 4, y: 4 (y_hi: 2, y_lo: 2; y = y_hi * 2 + y_lo), z: 4, core: 2. Of those that a mesh axis runs over, the one named last changes fastest.
Arguments:
- pressure: float32 [16, 512, 4096], P(None, 'gy', 'gx'), may hold values from -6 to 6
- vel_x: float32 [16, 512, 4096], P(None, 'gy', 'gx'), may hold values from -3 to 3
- vel_y: float32 [16, 512, 4096], P(None, 'gy', 'gx'), may hold values from -3 to 3
- vel_z: float32 [16, 512, 4096], P(None, 'gy', 'gx'), may hold values from -3 to 3
- memory_one: float32 [16, 512, 4096], P(None, 'gy', 'gx'), may hold values from -6 to 6
- memory_two: float32 [16, 512, 4096], P(None, 'gy', 'gx'), may hold values from -6 to 6
- density: float32 [16, 512, 4096], P(None, 'gy', 'gx'), may hold values from 0.6 to 1.8
- sound_speed: float32 [16, 512, 4096], P(None, 'gy', 'gx'), may hold values from 0.15 to 0.45
- tile_row: int32 [4, 32, 512], P('gy', 'gx'), may hold values from 0 to 2047
- tile_owner: int32 [4, 32, 512, 1], P('gy', 'gx'), may hold values from 0 to 127; in each aligned block of 512 rows (0 to 511, 512 to 1023, ..., all dimensions but the last counted through in order) at most 8 rows name the same one
- src_cell: int32 [4, 32, 256], P('gy', 'gx'), may hold values from 0 to 262143
- src_wave: float32 [4, 32, 4, 256], P('gy', 'gx'), may hold values from -6 to 6
Outputs:
- pressure_out: float32 [16, 512, 4096], P(None, 'gy', 'gx')
- vel_x_out: float32 [16, 512, 4096], P(None, 'gy', 'gx')
- vel_y_out: float32 [16, 512, 4096], P(None, 'gy', 'gx')
- vel_z_out: float32 [16, 512, 4096], P(None, 'gy', 'gx')
- memory_one_out: float32 [16, 512, 4096], P(None, 'gy', 'gx')
- memory_two_out: float32 [16, 512, 4096], P(None, 'gy', 'gx')
- farfield: float32 [2, 16384], P(None, ('gx', 'gy'))
The draws below stay inside these ranges and needn't reach their ends.
Inputs may be any that keep to these rules, and one draw needn't show every extreme that they name: `tile_owner`: in the tiles of one device, at most 8 have the same owner, and some owner has exactly 8 of them; every device owns some tile.
All inputs are finite; a program needn't handle non-finite values.
Results may differ from the reference program's by a relative error of at most 0.0003.
Values sent between devices are 32-bit elements; how exact they have to be, the bound alone decides.
A program may use at most 128 MiB of HBM per device.

```python
import math
import jax
import jax.numpy as jnp
import numpy as np
from jax import lax

CX = 128
CY = 128
NZ = 16
TSLOT = 512
NSRC = 256
STEPS = 4
ANG_DEV = 128
WAVELEN = 16
NX = 4096
NY = 512
ANGLES = 16384
CAP = 8
PERIOD = 4096
N_GX = 32
N_GY = 4
DEVICES = 128


def with_ends(values, key, least, largest):
    spot = [jax.random.randint(jax.random.fold_in(key, axis), (), 0, length) for axis, length in enumerate(values.shape)]
    main_axis = values.shape.index(max(values.shape))
    neighbour = spot[:main_axis] + [(spot[main_axis] + 1) % values.shape[main_axis]] + spot[main_axis + 1:]
    return values.at[tuple(spot)].set(least).at[tuple(neighbour)].set(largest)


def steps_of(key, dims, cuts, smallest, high):
    def one(axis_at, shards_of):
        heights = jax.random.uniform(jax.random.fold_in(jax.random.fold_in(key, 6), axis_at), (shards_of,), jnp.float32, smallest / len(cuts), high / len(cuts))
        return jnp.repeat(jnp.exp(heights), dims[axis_at] // shards_of).reshape((-1,) + (1,) * (len(dims) - axis_at - 1))

    gain = one(*cuts[0])
    for cut in cuts[1:]:
        gain = gain * one(*cut)
    return gain


def shared_out(rng, own, number, rows, amount, top, reach, lean):
    ranking = jax.random.permutation(rng, amount)
    packed, common = shares(amount, rows * top, reach, lean, True), shares(amount, rows * top, reach, lean, False)
    places = jnp.arange(amount)

    def named(tallies, turn):
        used = int((tallies > 0).sum())
        fixed = max(1, used // 4)
        passed = fixed + (places - fixed + turn * (used - fixed)) % max(1, amount - fixed)
        return jnp.zeros((amount,), jnp.int32).at[ranking[jnp.where(places < fixed, places, passed)]].set(jnp.asarray(tallies, jnp.int32))

    tallies = jnp.where(number % 4 == 0, named(packed, number // 4), named(common, number - number // 4 - 1))
    mixed = jax.random.permutation(jax.random.fold_in(own, 3), amount)
    donor, receiver = mixed[0:amount // 2 * 2:2], mixed[1:amount // 2 * 2:2]
    margin = jnp.minimum(tallies[donor] - 1, reach - tallies[receiver]) // 2
    margin = jnp.where((donor == ranking[0]) | (receiver == ranking[0]) | (tallies[receiver] == 0), 0, jnp.maximum(margin, 0))
    passed = jax.random.randint(jax.random.fold_in(own, 4), (amount // 2,), 0, 1 << 20) % (margin + 1)
    tallies = tallies.at[donor].add(-passed).at[receiver].add(passed)
    items = jnp.searchsorted(jnp.cumsum(tallies), jnp.arange(rows * top), side="right").astype(jnp.int32)
    table = items.reshape(top, rows).T
    table = table[jax.random.permutation(jax.random.fold_in(own, 1), rows)]
    turn = jax.random.randint(jax.random.fold_in(own, 2), (rows, 1), 0, top)
    return jnp.take_along_axis(table, (jnp.arange(top)[None, :] + turn) % top, axis=1)


def shares(count, total, most, slope, full):
    loads = [(1 << 20) // math.isqrt(grade ** slope) + 1 for grade in range(1, count + 1)]
    largest = most if full else min(most, max(-(-total // count), total * loads[0] // sum(loads)))
    least = 1 if total - largest >= count - 1 else 0
    holding, surplus = [largest] + [least] * (count - 1), total - largest - least * (count - 1)
    while surplus > 0:
        free = [i for i in range(1, count) if holding[i] < largest] or [i for i in range(1, count) if holding[i] < most]
        mass, remaining = sum([loads[i] for i in free]), surplus
        for i in free:
            extra = min(most - holding[i], max(1, remaining * loads[i] // mass), surplus)
            holding[i] = holding[i] + extra
            surplus = surplus - extra
    return np.array(holding)


def gaussian(stream_key, dims, spread, reach, pieces=(), kind=jnp.bfloat16):
    factor_of = steps_of(stream_key, dims, pieces, -0.22, 0.18) if pieces else 1.0
    values = jax.random.normal(stream_key, dims, jnp.float32) * spread * factor_of
    return jnp.minimum(jnp.maximum(values, -reach), reach).astype(kind)


def setup_inputs(seed: int = 0) -> dict:
    key_list = jax.random.split(jax.random.key(seed), 13)
    pressure = gaussian(key_list[0], (NZ, NY, NX), 1.0, 6.0, ((1, 4), (2, 32)), jnp.float32)
    vel_x = gaussian(key_list[1], (NZ, NY, NX), 0.5, 3.0, ((1, 4), (2, 32)), jnp.float32)
    vel_y = gaussian(key_list[2], (NZ, NY, NX), 0.5, 3.0, ((1, 4), (2, 32)), jnp.float32)
    vel_z = gaussian(key_list[3], (NZ, NY, NX), 0.5, 3.0, ((1, 4), (2, 32)), jnp.float32)
    memory_one = gaussian(key_list[4], (NZ, NY, NX), 1.0, 6.0, ((1, 4), (2, 32)), jnp.float32)
    memory_two = gaussian(key_list[5], (NZ, NY, NX), 1.0, 6.0, ((1, 4), (2, 32)), jnp.float32)
    density = jnp.clip(jnp.exp(math.log(1.8) - 1.0986122 * jax.random.uniform(key_list[6], (NZ, NY, NX), jnp.float32) ** steps_of(key_list[6], (NZ, NY, NX), ((1, 4), (2, 32)), -0.2, 0.2)), 0.6, 1.8)
    sound_speed = jnp.clip(jnp.exp(math.log(0.45) - 1.0986122 * jax.random.uniform(key_list[7], (NZ, NY, NX), jnp.float32) ** steps_of(key_list[7], (NZ, NY, NX), ((1, 4), (2, 32)), -0.2, 0.2)), 0.15, 0.45)
    tile_row = with_ends(jax.random.randint(key_list[8], (N_GY, N_GX, TSLOT), 0, NZ * CY), jax.random.fold_in(key_list[8], 1), 0, (NZ * CY) - 1).astype(jnp.int32)
    tile_owner_keys = jax.random.split(jax.random.fold_in(key_list[9], 1), N_GY * N_GX * TSLOT // TSLOT)
    tile_owner_turns = jax.random.permutation(jax.random.fold_in(key_list[9], 3), N_GY * N_GX * TSLOT // TSLOT)
    tile_owner = jax.vmap(lambda own, number: shared_out(jax.random.fold_in(key_list[9], 2), own, number, TSLOT, DEVICES, 1, CAP, 2))(tile_owner_keys, tile_owner_turns).reshape((N_GY, N_GX, TSLOT, 1))
    src_cell = with_ends(jax.random.randint(key_list[10], (N_GY, N_GX, NSRC), 0, NZ * CY * CX), jax.random.fold_in(key_list[10], 1), 0, (NZ * CY * CX) - 1).astype(jnp.int32)
    src_wave = gaussian(key_list[11], (N_GY, N_GX, STEPS, NSRC), 1.0, 6.0, ((0, 4), (1, 32)), jnp.float32)
    return dict(pressure=pressure, vel_x=vel_x, vel_y=vel_y, vel_z=vel_z, memory_one=memory_one, memory_two=memory_two, density=density, sound_speed=sound_speed, tile_row=tile_row, tile_owner=tile_owner, src_cell=src_cell, src_wave=src_wave)


coef_near = 9.0 / 8.0
coef_far = 1.0 / 24.0
relax_one = 0.6
feed_one = 0.06
relax_two = 0.9
feed_two = 0.025
step_phase = 0.7
impedance = 0.35

def shifted(padded, dimension, offset, length):
    return lax.slice_in_dim(padded, 2 + offset, 2 + offset + length, axis=dimension)

def forward(padded, dimension, length):
    return coef_near * (shifted(padded, dimension, 1, length) - shifted(padded, dimension, 0, length)) - coef_far * (shifted(padded, dimension, 2, length) - shifted(padded, dimension, -1, length))

def backward(padded, dimension, length):
    return coef_near * (shifted(padded, dimension, 0, length) - shifted(padded, dimension, -1, length)) - coef_far * (shifted(padded, dimension, 1, length) - shifted(padded, dimension, -2, length))

def padding(field, dimension):
    widths = [(0, 0), (0, 0), (0, 0)]
    widths[dimension] = (2, 2)
    return jnp.pad(field, widths)

def reference(pressure, vel_x, vel_y, vel_z, memory_one, memory_two, density, sound_speed, tile_row, tile_owner, src_cell, src_wave):
    modulus = density * sound_speed * sound_speed
    buoyancy = 1.0 / density
    index_y = jnp.arange(N_GY, dtype=jnp.int32)[:, None, None]
    index_x = jnp.arange(N_GX, dtype=jnp.int32)[None, :, None]
    layer = src_cell // (CY * CX)
    global_y = index_y * CY + src_cell // CX % CY
    global_x = index_x * CX + src_cell % CX
    flat_cells = ((layer * NY + global_y) * NX + global_x).reshape(-1)
    spectra = [jnp.zeros_like(pressure) for number in range(4)]
    for moment in range(STEPS):
        vel_x = vel_x - buoyancy * forward(padding(pressure, 2), 2, NX)
        vel_y = vel_y - buoyancy * forward(padding(pressure, 1), 1, NY)
        vel_z = vel_z - buoyancy * forward(padding(pressure, 0), 0, NZ)
        divergence = backward(padding(vel_x, 2), 2, NX) + backward(padding(vel_y, 1), 1, NY) + backward(padding(vel_z, 0), 0, NZ)
        memory_one = relax_one * memory_one + feed_one * divergence
        memory_two = relax_two * memory_two + feed_two * divergence
        pressure = pressure - modulus * (divergence - memory_one - memory_two)
        pressure = pressure.reshape(-1).at[flat_cells].add(src_wave[:, :, moment, :].reshape(-1)).reshape(NZ, NY, NX)
        weight_cos = math.cos(step_phase * (moment + 1))
        weight_sin = math.sin(step_phase * (moment + 1))
        spectra = [spectra[0] + weight_cos * pressure, spectra[1] + weight_sin * pressure, spectra[2] + weight_cos * vel_z, spectra[3] + weight_sin * vel_z]
    wave_scale = 2.0 * math.pi / PERIOD
    magnitude = 2.0 * math.pi / WAVELEN
    wave_x = 2 * jnp.arange(ANG_DEV, dtype=jnp.int32) + 1 - ANG_DEV

    def one_source(total, source):
        column = source // N_GY
        row_tile = source % N_GY
        tile_rows = tile_row[row_tile, column]
        owners = tile_owner[row_tile, column, :, 0]
        blocks = [lax.dynamic_slice(field, (jnp.int32(0), row_tile * CY, column * CX), (NZ, CY, CX)).reshape(NZ * CY, CX)[tile_rows] for field in spectra]
        layer_z = tile_rows // CY
        tile_y = row_tile * CY + tile_rows % CY
        tile_x = column * CX + jnp.arange(CX, dtype=jnp.int32)
        wave_y = 2 * owners + 1 - DEVICES
        phase_int = (wave_x[None, :, None] * tile_x[None, None, :] + (wave_y * tile_y)[:, None, None]) % PERIOD
        scaled_x = wave_scale * wave_x
        scaled_y = wave_scale * wave_y
        wave_z = jnp.sqrt(magnitude * magnitude - (scaled_x * scaled_x)[None, :] - (scaled_y * scaled_y)[:, None])
        cosine_z = wave_z / magnitude
        phase = wave_scale * phase_int + (wave_z * layer_z[:, None])[:, :, None]
        q_real = cosine_z[:, :, None] * blocks[0][:, None, :] + impedance * blocks[2][:, None, :]
        q_imag = cosine_z[:, :, None] * blocks[1][:, None, :] + impedance * blocks[3][:, None, :]
        cos_phase = jnp.cos(phase)
        sin_phase = jnp.sin(phase)
        real_part = lax.optimization_barrier(jnp.sum(cos_phase * q_real + sin_phase * q_imag, axis=2))
        imag_part = lax.optimization_barrier(jnp.sum(cos_phase * q_imag - sin_phase * q_real, axis=2))
        contrib = jnp.stack([real_part, imag_part], axis=1)
        return (total + jax.ops.segment_sum(contrib, owners, num_segments=DEVICES), None)
    start = jnp.zeros((DEVICES, 2, ANG_DEV), jnp.float32)
    total, unused = lax.scan(one_source, start, jnp.arange(DEVICES, dtype=jnp.int32))
    farfield = jnp.transpose(total, (1, 0, 2)).reshape(2, ANGLES) * (1.0 / math.sqrt(TSLOT * CX))
    return (pressure, vel_x, vel_y, vel_z, memory_one, memory_two, farfield)
```

```python
import functools
import math

import jax
import jax.numpy as jnp
import numpy as np
from jax import lax
from jax.experimental import pallas as pl
from jax.experimental.pallas import tpu as pltpu
from jax.sharding import PartitionSpec as P

MESH = pl.DeviceIdType.MESH
F32 = jnp.float32
BF16 = jnp.bfloat16

ANG = 128
WAVELEN = 16
C1 = 9.0 / 8.0
C2 = 1.0 / 24.0
RELAX1, FEED1 = 0.6, 0.06
RELAX2, FEED2 = 0.9, 0.025
STEP_PHASE = 0.7
IMPEDANCE = 0.35

STEPS = 4
NZ, CY, CX = 16, 128, 128
TILES = 512
SRCS = 256
PAD = 16
ROWS = PAD + CY + 16
CHUNK = 32
NG = 4
GZ = NZ // NG
XOUT = 4
LOW_X, HIGH_X, LOW_Y, HIGH_Y = 0, 1, 2, 3


def split2(value):
    high = value.astype(BF16)
    low = (value - high.astype(F32)).astype(BF16)
    return high, low


def split3(value):
    high = value.astype(BF16)
    rest = value - high.astype(F32)
    mid = rest.astype(BF16)
    low = (rest - mid.astype(F32)).astype(BF16)
    return high, mid, low


def dot(a, b):
    return lax.dot_general(a, b, (((1,), (0,)), ((), ())), preferred_element_type=F32)


def dot_nt(a, b):
    return lax.dot_general(a, b, (((1,), (1,)), ((), ())), preferred_element_type=F32)


def sincos_turns(turns):
    f = turns - jnp.floor(turns + 0.5)
    quad = jnp.floor(f * 4.0 + 0.5)
    x = (f - quad * 0.25) * (2.0 * math.pi)
    x2 = x * x
    s = x * (1.0 + x2 * (-1.0 / 6 + x2 * (1.0 / 120 + x2 * (-1.0 / 5040 + x2 * (1.0 / 362880)))))
    c = 1.0 + x2 * (-0.5 + x2 * (1.0 / 24 + x2 * (-1.0 / 720 + x2 * (1.0 / 40320))))
    swap = jnp.abs(quad) == 1.0
    a = jnp.where(swap, s, c)
    b = jnp.where(swap, c, s)
    cos_sign = jnp.where((quad == 0.0) | (quad == -1.0), 1.0, -1.0)
    sin_sign = jnp.where((quad == 0.0) | (quad == 1.0), 1.0, -1.0)
    return a * cos_sign, b * sin_sign


def unroll_shift(block):
    return (128 - (8 * block + 3)) % 128


def pack_rows(read, group):
    packed = jnp.zeros((8, 128), F32)
    for block in range(16):
        rolled = pltpu.roll(read(block), (8 * block + 3) % 128, 1)
        packed = jnp.where(group == block, rolled, packed)
    return packed


def kernel(
    nx,
    ny,
    p_in,
    vx_in,
    vy_in,
    vz_in,
    m1_in,
    m2_in,
    de_in,
    cs_in,
    row_s,
    row_v,
    own_v,
    cell_v,
    wave_v,
    thi,
    tlo,
    p_out,
    vx_out,
    vy_out,
    vz_out,
    m1_out,
    m2_out,
    ff_out,
    P_,
    VX,
    VY,
    VZ,
    M1,
    M2,
    B,
    MOD,
    CS,
    SRC,
    PO,
    PH,
    XO,
    XH,
    TAB,
    HOT,
    G,
    RA,
    RB,
    RC,
    ld_sem,
    st_sem,
    snd,
    rcv,
    snd0,
    rcv0,
    sa,
    ra,
    sb,
    rb,
    sc,
    rc,
):
    gx = lax.axis_index("gx")
    gy = lax.axis_index("gy")
    devices = nx * ny
    period = 2 * WAVELEN * max(ANG, devices)
    inner = nx // XOUT
    xo, xi = gx // inner, gx % inner
    has = [gx > 0, gx < nx - 1, gy > 0, gy < ny - 1]
    peer = [{"gx": gx - 1}, {"gx": gx + 1}, {"gy": gy - 1}, {"gy": gy + 1}]
    peers_a = [{"gy": (gy + k) % ny} for k in range(1, ny)]
    peers_b = [{"gx": (xo + k) % XOUT * inner + xi} for k in range(1, XOUT)]
    peers_c = [{"gx": xo * inner + (xi + k) % inner} for k in range(1, inner)]

    dst = [
        P_.at[0, pl.ds(1, NZ), pl.ds(PAD, CY), :],
        VX,
        VY.at[:, pl.ds(PAD, CY), :],
        VZ.at[0, pl.ds(2, NZ)],
        M1,
        M2,
        B.at[:, pl.ds(PAD, CY), :],
        CS,
    ]
    src = [p_in, vx_in, vy_in, vz_in, m1_in, m2_in, de_in, cs_in]
    loads = [pltpu.make_async_copy(src[i], dst[i], ld_sem.at[i]) for i in range(8)]
    for i in (0, 1, 6, 7, 2, 3, 4, 5):
        loads[i].start()

    barrier = pltpu.get_barrier_semaphore()
    for d in range(4):

        @pl.when(has[d])
        def _():
            pl.semaphore_signal(barrier, inc=1, device_id=peer[d], device_id_type=MESH)

    for target in peers_a + peers_b + peers_c:
        pl.semaphore_signal(barrier, inc=1, device_id=target, device_id_type=MESH)
    fixed = len(peers_a) + len(peers_b) + len(peers_c)
    neighbours = sum(jnp.where(flag, 1, 0) for flag in has)
    pl.semaphore_wait(barrier, fixed + neighbours)

    lane = lax.broadcasted_iota(jnp.int32, (8, 128), 1)
    group = lane >> 3
    from_low = (lane & 7) < 3

    def rim_copy(s, g, d):
        z0 = g * GZ
        if d in (LOW_X, HIGH_X):
            source = PO.at[s, pl.ds(z0, GZ)]
            target = PH.at[s, HIGH_X if d == LOW_X else LOW_X, pl.ds(z0, GZ)]
        else:
            y_from, y_to = (PAD, PAD + CY) if d == LOW_Y else (PAD + CY - 8, PAD - 8)
            source = P_.at[s, pl.ds(z0 + 1, GZ), pl.ds(y_from, 8), :]
            target = P_.at[s, pl.ds(z0 + 1, GZ), pl.ds(y_to, 8), :]
        back = {LOW_X: HIGH_X, HIGH_X: LOW_X, LOW_Y: HIGH_Y, HIGH_Y: LOW_Y}[d]
        return pltpu.make_async_remote_copy(
            src_ref=source,
            dst_ref=target,
            send_sem=snd.at[s, g, d],
            recv_sem=rcv.at[s, g, back],
            device_id=peer[d],
            device_id_type=MESH,
        )

    def send_rims(s, g):
        for d in range(4):

            @pl.when(has[d])
            def _():
                rim_copy(s, g, d).start()

    def wait_rims(s, g):
        for d in range(4):

            @pl.when(has[d])
            def _():
                back = {LOW_X: HIGH_X, HIGH_X: LOW_X, LOW_Y: HIGH_Y, HIGH_Y: LOW_Y}[d]
                rim_copy(s, g, back).wait_recv()

    def first_copies(d):
        back = {LOW_X: HIGH_X, HIGH_X: LOW_X, LOW_Y: HIGH_Y, HIGH_Y: LOW_Y}[d]
        if d in (LOW_X, HIGH_X):
            pairs = [(XO, XH.at[back])]
        else:
            y_from, y_to = (0, PAD + CY) if d == LOW_Y else (CY - 8, PAD - 8)
            pairs = [
                (vy_in.at[:, pl.ds(y_from, 8), :], VY.at[:, pl.ds(y_to, 8), :]),
                (de_in.at[:, pl.ds(y_from, 8), :], B.at[:, pl.ds(y_to, 8), :]),
            ]
        return [
            pltpu.make_async_remote_copy(
                src_ref=a,
                dst_ref=b,
                send_sem=snd0.at[d, i],
                recv_sem=rcv0.at[back, i],
                device_id=peer[d],
                device_id_type=MESH,
            )
            for i, (a, b) in enumerate(pairs)
        ]

    loads[0].wait()

    def pack_first(z, carry):
        PO[0, z] = pack_rows(lambda k: P_[0, z + 1, PAD + 8 * k : PAD + 8 * k + 8, :], group)
        return carry

    for g in range(NG):
        lax.fori_loop(g * GZ, (g + 1) * GZ, pack_first, 0)
        send_rims(0, g)
    for d in (LOW_Y, HIGH_Y):

        @pl.when(has[d])
        def _():
            for copy in first_copies(d):
                copy.start()

    loads[1].wait()
    loads[6].wait()

    def pack_others(z, carry):
        XO[0, z] = pack_rows(lambda k: VX[z, 8 * k : 8 * k + 8, :], group)
        XO[1, z] = pack_rows(lambda k: B[z, PAD + 8 * k : PAD + 8 * k + 8, :], group)
        return carry

    lax.fori_loop(0, NZ, pack_others, 0)
    for d in (LOW_X, HIGH_X):

        @pl.when(has[d])
        def _():
            for copy in first_copies(d):
                copy.start()

    plane = jnp.zeros((CY, CX), F32)
    for s in range(STEPS):
        for z in (0, NZ + 1, NZ + 2):
            P_[s, z, PAD : PAD + CY, :] = plane
        for z in (0, 1, NZ + 2):
            VZ[s + 1, z] = plane
    rim = jnp.zeros((NZ, 8, 128), F32)
    for d in (LOW_X, HIGH_X):

        @pl.when(jnp.logical_not(has[d]))
        def _():
            for s in range(STEPS):
                PH[s, d] = rim
            XH[d, 0] = rim
            XH[d, 1] = rim + 1.0

    for d, y0 in ((LOW_Y, PAD - 8), (HIGH_Y, PAD + CY)):

        @pl.when(jnp.logical_not(has[d]))
        def _():
            for s in range(STEPS):
                P_[s, 1 : NZ + 1, y0 : y0 + 8, :] = rim
            VY[:, y0 : y0 + 8, :] = rim

    cells = cell_v[...]
    src_row = cells >> 7
    src_lane = cells & 127
    lane_hot = lax.broadcasted_iota(jnp.int32, (CX, SRCS), 0) == src_lane
    parts = []
    for s in range(STEPS):
        parts.append(split3(jnp.where(lane_hot, wave_v[s : s + 1, :], 0.0)))
    right = [jnp.concatenate([parts[s][i] for s in range(STEPS)], axis=0) for i in range(3)]
    for i in range(3):
        HOT[i] = right[i]

    def sources(z, carry):
        rows = lax.broadcasted_iota(jnp.int32, (CY, SRCS), 0) + z * CY
        hot = jnp.where(rows == src_row, 1.0, 0.0).astype(BF16)
        total = dot_nt(hot, HOT[0]) + dot_nt(hot, HOT[1]) + dot_nt(hot, HOT[2])
        for s in range(STEPS):
            SRC[s, z] = total[:, s * CX : (s + 1) * CX]
        return carry

    lax.fori_loop(0, NZ, sources, 0)

    scale = 2.0 * math.pi / period
    magnitude = 2.0 * math.pi / WAVELEN
    angle = lax.broadcasted_iota(jnp.int32, (128, ANG), 1)
    wave_x = (2 * angle + 1 - ANG).astype(F32)
    x_turn = wave_x * (gx * CX).astype(F32)
    kx2 = (scale * wave_x) * (scale * wave_x)
    for k in range(TILES // 128):
        own = jnp.broadcast_to(own_v[:, k * 128 : (k + 1) * 128].astype(F32), (128, 128)).T
        row = jnp.broadcast_to(row_v[:, k * 128 : (k + 1) * 128].astype(F32), (128, 128)).T
        layer = jnp.floor(row * (1.0 / CY))
        tile_y = row - layer * CY + (gy * CY).astype(F32)
        wave_y = 2.0 * own + (1.0 - devices)
        ky = scale * wave_y
        wave_z = jnp.sqrt(magnitude * magnitude - kx2 - ky * ky)
        whole = (x_turn + wave_y * tile_y) * (1.0 / period)
        turns = (whole - jnp.floor(whole)) + wave_z * layer * (1.0 / (2.0 * math.pi))
        cosine, sine = sincos_turns(turns)
        TAB[0, k * 128 : (k + 1) * 128, :] = cosine
        TAB[1, k * 128 : (k + 1) * 128, :] = sine
        TAB[2, k * 128 : (k + 1) * 128, :] = wave_z * (1.0 / magnitude)

    for i in (7, 2, 3, 4, 5):
        loads[i].wait()
    for d in range(4):

        @pl.when(has[d])
        def _():
            back = {LOW_X: HIGH_X, HIGH_X: LOW_X, LOW_Y: HIGH_Y, HIGH_Y: LOW_Y}[d]
            for copy in first_copies(back):
                copy.wait_recv()

    low_ok = jnp.where(has[LOW_X], 1.0, 0.0)
    high_ok = jnp.where(has[HIGH_X], 1.0, 0.0)

    def material(z, carry):
        for y0 in range(0, CY, CHUNK):
            rho = B[z, PAD + y0 : PAD + y0 + CHUNK, :]
            speed = CS[z, y0 : y0 + CHUNK, :]
            MOD[z, y0 : y0 + CHUNK, :] = rho * speed * speed
            B[z, PAD + y0 : PAD + y0 + CHUNK, :] = 1.0 / rho
        XO[0, z] = jnp.where(from_low, XH[LOW_X, 0, z], XH[HIGH_X, 0, z])
        XO[1, z] = jnp.where(
            from_low, low_ok / XH[LOW_X, 1, z], high_ok / XH[HIGH_X, 1, z]
        )
        return carry

    for d in (LOW_X, HIGH_X):

        @pl.when(has[d])
        def _():
            for copy in first_copies(d):
                copy.wait_send()

    lax.fori_loop(0, NZ, material, 0)
    for d, y0 in ((LOW_Y, PAD - 8), (HIGH_Y, PAD + CY)):

        @pl.when(has[d])
        def _():
            B[:, y0 : y0 + 8, :] = 1.0 / B[:, y0 : y0 + 8, :]

        @pl.when(jnp.logical_not(has[d]))
        def _():
            B[:, y0 : y0 + 8, :] = rim

    wide = lax.broadcasted_iota(jnp.int32, (CHUNK, 128), 1)

    def velocities(s, z):
        near = jnp.where(from_low, PH[s, LOW_X, z], PH[s, HIGH_X, z])
        mine = PO[s, z]
        low = jnp.where(from_low, near, mine)
        high = jnp.where(from_low, mine, near)

        def along(v):
            return C1 * (pltpu.roll(v, 127, 1) - v) - C2 * (
                pltpu.roll(v, 126, 1) - pltpu.roll(v, 1, 1)
            )

        XO[0, z] = XO[0, z] - XO[1, z] * jnp.where(from_low, along(low), along(high))
        for y0 in (PAD - 8, PAD + CY):
            f = C1 * (P_[s, z + 1, y0 + 1 : y0 + 9, :] - P_[s, z + 1, y0 : y0 + 8, :]) - C2 * (
                P_[s, z + 1, y0 + 2 : y0 + 10, :] - P_[s, z + 1, y0 - 1 : y0 + 7, :]
            )
            VY[z, y0 : y0 + 8, :] = VY[z, y0 : y0 + 8, :] - B[z, y0 : y0 + 8, :] * f
        for y0 in range(0, CY, CHUNK):
            r = PAD + y0
            e = r + CHUNK
            p = P_[s, z + 1, r:e, :]
            b = B[z, r:e, :]
            halo = jnp.concatenate(
                [pltpu.roll(near, unroll_shift(y0 // 8 + i), 1) for i in range(CHUNK // 8)], axis=0
            )
            left = jnp.where(wide == 127, halo, p)
            next_ = jnp.where(wide == 0, halo, p)
            after = jnp.where(wide < 2, halo, p)
            f = C1 * (pltpu.roll(next_, 127, 1) - p) - C2 * (
                pltpu.roll(after, 126, 1) - pltpu.roll(left, 1, 1)
            )
            VX[z, y0 : y0 + CHUNK, :] = VX[z, y0 : y0 + CHUNK, :] - b * f
            f = C1 * (P_[s, z + 1, r + 1 : e + 1, :] - p) - C2 * (
                P_[s, z + 1, r + 2 : e + 2, :] - P_[s, z + 1, r - 1 : e - 1, :]
            )
            VY[z, r:e, :] = VY[z, r:e, :] - b * f
            f = C1 * (P_[s, z + 2, r:e, :] - p) - C2 * (P_[s, z + 3, r:e, :] - P_[s, z, r:e, :])
            VZ[s + 1, z + 2, y0 : y0 + CHUNK, :] = VZ[s, z + 2, y0 : y0 + CHUNK, :] - b * f

    def pressures(s, z):
        near = XO[0, z]
        packed = jnp.zeros((8, 128), F32)
        for y0 in range(0, CY, CHUNK):
            r = PAD + y0
            e = r + CHUNK
            halo = jnp.concatenate(
                [pltpu.roll(near, unroll_shift(y0 // 8 + i), 1) for i in range(CHUNK // 8)], axis=0
            )
            v = VX[z, y0 : y0 + CHUNK, :]
            left = jnp.where(wide == 127, halo, v)
            before = jnp.where(wide >= 126, halo, v)
            next_ = jnp.where(wide == 0, halo, v)
            div = C1 * (v - pltpu.roll(left, 1, 1)) - C2 * (
                pltpu.roll(next_, 127, 1) - pltpu.roll(before, 2, 1)
            )
            div = div + (
                C1 * (VY[z, r:e, :] - VY[z, r - 1 : e - 1, :])
                - C2 * (VY[z, r + 1 : e + 1, :] - VY[z, r - 2 : e - 2, :])
            )
            q, t = y0, y0 + CHUNK
            div = div + (
                C1 * (VZ[s + 1, z + 2, q:t, :] - VZ[s + 1, z + 1, q:t, :])
                - C2 * (VZ[s + 1, z + 3, q:t, :] - VZ[s + 1, z, q:t, :])
            )
            one = RELAX1 * M1[z, q:t, :] + FEED1 * div
            two = RELAX2 * M2[z, q:t, :] + FEED2 * div
            M1[z, q:t, :] = one
            M2[z, q:t, :] = two
            new = P_[s, z + 1, r:e, :] - MOD[z, q:t, :] * (div - one - two) + SRC[s, z, q:t, :]
            P_[s + 1, z + 1, r:e, :] = new
            for i in range(CHUNK // 8):
                block = y0 // 8 + i
                rolled = pltpu.roll(new[8 * i : 8 * i + 8, :], (8 * block + 3) % 128, 1)
                packed = jnp.where(group == block, rolled, packed)
        PO[s + 1, z] = packed

    def stores(g):
        zs = pl.ds(g * GZ, GZ)
        pairs = [
            (P_.at[STEPS, pl.ds(g * GZ + 1, GZ), pl.ds(PAD, CY), :], p_out.at[zs]),
            (VX.at[zs], vx_out.at[zs]),
            (VY.at[zs, pl.ds(PAD, CY), :], vy_out.at[zs]),
            (VZ.at[STEPS, pl.ds(g * GZ + 2, GZ)], vz_out.at[zs]),
            (M1.at[zs], m1_out.at[zs]),
            (M2.at[zs], m2_out.at[zs]),
        ]
        return [pltpu.make_async_copy(a, b, st_sem.at[g, i]) for i, (a, b) in enumerate(pairs)]

    def step(s, carry):
        def planes(z, inner_carry):
            @pl.when(z < NZ)
            def _():
                @pl.when(z % GZ == 0)
                def _():
                    wait_rims(s, z // GZ)

                velocities(s, z)

            @pl.when(z > 0)
            def _():
                pressures(s, z - 1)

                @pl.when(z % GZ == 0)
                def _():
                    g = z // GZ - 1

                    @pl.when(s < STEPS - 1)
                    def _():
                        send_rims(s + 1, g)

                    @pl.when(s == STEPS - 1)
                    def _():
                        for copy in stores(g):
                            copy.start()

            return inner_carry

        return lax.fori_loop(0, NZ + 1, planes, carry)

    lax.fori_loop(0, STEPS, step, 0)

    def gather(t, carry):
        r = row_s[t]
        z = r >> 7
        y = r & 127
        for s in range(STEPS):
            G[s, pl.ds(t, 1), :] = P_[s + 1, z + 1, pl.ds(y + PAD, 1), :]
            G[STEPS + s, pl.ds(t, 1), :] = VZ[s + 1, z + 2, pl.ds(y, 1), :]
        return carry

    lax.fori_loop(0, TILES, gather, 0, unroll=8)

    weights = [(math.cos(STEP_PHASE * (s + 1)), math.sin(STEP_PHASE * (s + 1))) for s in range(STEPS)]
    own_row = own_v[...]
    order = (own_row % ny) * nx + own_row // ny
    hot = jnp.where(
        lax.broadcasted_iota(jnp.int32, (devices, TILES), 0) == order, 1.0, 0.0
    ).astype(BF16)
    total = jnp.zeros((devices, 2 * ANG), F32)
    for k in range(TILES // 128):
        t0, t1 = k * 128, (k + 1) * 128

        def mixed(base):
            fields = [G[base + s, t0:t1, :] for s in range(STEPS)]
            real = sum(weights[s][0] * fields[s] for s in range(STEPS))
            imag = sum(weights[s][1] * fields[s] for s in range(STEPS))
            high, low = split2(jnp.concatenate([real, imag], axis=1))
            return dot(high, thi[...]) + dot(low, thi[...]) + dot(high, tlo[...])

        press = mixed(0)
        flow = mixed(STEPS)
        cosine, sine, lift = TAB[0, t0:t1, :], TAB[1, t0:t1, :], TAB[2, t0:t1, :]
        real = lift * press[:, :ANG] + IMPEDANCE * flow[:, :ANG]
        imag = lift * press[:, ANG:] + IMPEDANCE * flow[:, ANG:]
        both = jnp.concatenate([cosine * real + sine * imag, cosine * imag - sine * real], axis=1)
        high, low = split2(both)
        total = total + (dot(hot[:, t0:t1], high) + dot(hot[:, t0:t1], low))
    for j in range(ny):
        RA[ny + j] = total[j * nx : (j + 1) * nx, :]

    def exchange(targets, source_of, slots, send, recv):
        copies = []
        for k, target in enumerate(targets):
            copy = pltpu.make_async_remote_copy(
                src_ref=source_of(k + 1),
                dst_ref=slots.at[k + 1],
                send_sem=send.at[k],
                recv_sem=recv.at[k],
                device_id=target,
                device_id_type=MESH,
            )
            copy.start()
            copies.append(copy)
        return copies

    copies = exchange(peers_a, lambda k: RA.at[ny + (gy + k) % ny], RA, sa, ra)
    part = RA[ny + gy]
    for k, copy in enumerate(copies):
        copy.wait()
        part = part + RA[k + 1]
    for j in range(XOUT):
        RB[XOUT + j] = part[j * inner : (j + 1) * inner, :]
    copies = exchange(peers_b, lambda k: RB.at[XOUT + (xo + k) % XOUT], RB, sb, rb)
    part = RB[XOUT + xo]
    for k, copy in enumerate(copies):
        copy.wait()
        part = part + RB[k + 1]
    RC[0] = part
    copies = exchange(peers_c, lambda k: RC.at[0], RC, sc, rc)
    for k, copy in enumerate(copies):
        copy.wait()
        part = part + RC[k + 1]
    norm = 1.0 / math.sqrt(TILES * CX)
    keep = lax.broadcasted_iota(jnp.int32, (inner, 2 * ANG), 0) == xi
    final = jnp.sum(jnp.where(keep, part, 0.0), axis=0, keepdims=True) * norm
    ff_out[0:1, :] = final[:, :ANG]
    ff_out[1:2, :] = final[:, ANG:]

    def drain(i, carry):
        s, g = i // NG, i % NG
        for d in range(4):

            @pl.when(has[d])
            def _():
                rim_copy(s, g, d).wait_send()

        return carry

    lax.fori_loop(0, STEPS * NG, drain, 0)
    for d in (LOW_Y, HIGH_Y):

        @pl.when(has[d])
        def _():
            for copy in first_copies(d):
                copy.wait_send()

    for g in range(NG):
        for copy in stores(g):
            copy.wait()


def tables():
    period = 4096
    wave = 2 * np.arange(ANG) + 1 - ANG
    phase = 2.0 * np.pi * ((np.arange(CX)[:, None] * wave[None, :]) % period) / period
    c, s = np.cos(phase), np.sin(phase)
    table = np.concatenate(
        [np.concatenate([c, -s], axis=1), np.concatenate([s, c], axis=1)], axis=0
    ).astype(np.float32)
    high = table.astype(jnp.bfloat16)
    low = (table - high.astype(np.float32)).astype(jnp.bfloat16)
    return high, low


def local(nx, ny, *args):
    fields = args[:8]
    tile_row, tile_owner, src_cell, src_wave = args[8:]
    rows = tile_row.reshape(TILES)
    high, low = tables()
    block = jax.ShapeDtypeStruct((NZ, CY, CX), F32)
    anywhere = pl.BlockSpec(memory_space=pl.ANY)
    vmem = pl.BlockSpec(memory_space=pltpu.VMEM)
    smem = pl.BlockSpec(memory_space=pltpu.SMEM)
    dma = pltpu.SemaphoreType.DMA
    inner = nx // XOUT
    return pl.pallas_call(
        functools.partial(kernel, nx, ny),
        out_shape=[block] * 6 + [jax.ShapeDtypeStruct((2, ANG), F32)],
        in_specs=[anywhere] * 8 + [smem] + [vmem] * 6,
        out_specs=[anywhere] * 6 + [vmem],
        scratch_shapes=[
            pltpu.VMEM((STEPS + 1, NZ + 3, ROWS, CX), F32),
            pltpu.VMEM((NZ, CY, CX), F32),
            pltpu.VMEM((NZ, ROWS, CX), F32),
            pltpu.VMEM((STEPS + 1, NZ + 3, CY, CX), F32),
            pltpu.VMEM((NZ, CY, CX), F32),
            pltpu.VMEM((NZ, CY, CX), F32),
            pltpu.VMEM((NZ, ROWS, CX), F32),
            pltpu.VMEM((NZ, CY, CX), F32),
            pltpu.VMEM((NZ, CY, CX), F32),
            pltpu.VMEM((STEPS, NZ, CY, CX), F32),
            pltpu.VMEM((STEPS + 1, NZ, 8, CX), F32),
            pltpu.VMEM((STEPS, 2, NZ, 8, CX), F32),
            pltpu.VMEM((2, NZ, 8, CX), F32),
            pltpu.VMEM((2, 2, NZ, 8, CX), F32),
            pltpu.VMEM((3, TILES, ANG), F32),
            pltpu.VMEM((3, STEPS * CX, SRCS), BF16),
            pltpu.VMEM((2 * STEPS, TILES, CX), F32),
            pltpu.VMEM((2 * ny, nx, 2 * ANG), F32),
            pltpu.VMEM((2 * XOUT, inner, 2 * ANG), F32),
            pltpu.VMEM((inner, inner, 2 * ANG), F32),
            dma((8,)),
            dma((NG, 6)),
            dma((STEPS, NG, 4)),
            dma((STEPS, NG, 4)),
            dma((4, 2)),
            dma((4, 2)),
            dma((ny - 1,)),
            dma((ny - 1,)),
            dma((XOUT - 1,)),
            dma((XOUT - 1,)),
            dma((inner - 1,)),
            dma((inner - 1,)),
        ],
        compiler_params=pltpu.CompilerParams(
            collective_id=0, has_side_effects=True, vmem_limit_bytes=56 * 1024 * 1024
        ),
    )(
        *fields,
        rows,
        rows.reshape(1, TILES),
        tile_owner.reshape(1, TILES),
        src_cell.reshape(1, SRCS),
        src_wave.reshape(STEPS, SRCS),
        high,
        low,
    )


def solution(mesh):
    field = P(None, "gy", "gx")
    return jax.shard_map(
        functools.partial(local, mesh.shape["gx"], mesh.shape["gy"]),
        mesh=mesh,
        in_specs=(field,) * 8
        + (
            P("gy", "gx", None),
            P("gy", "gx", None, None),
            P("gy", "gx", None),
            P("gy", "gx", None, None),
        ),
        out_specs=(field,) * 6 + (P(None, ("gx", "gy")),),
        check_vma=False,
    )
```

```python
import functools
import math

import jax
import jax.numpy as jnp
import numpy as np
from jax import lax
from jax.experimental import pallas as pl
from jax.experimental.pallas import tpu as pltpu
from jax.sharding import PartitionSpec as P

MESH = pl.DeviceIdType.MESH
F32 = jnp.float32
BF16 = jnp.bfloat16

ANG = 128
WAVELEN = 16
UNIT = 1.0 / 24.0
NEAR = 27.0
RELAX1, FEED1 = 0.6, 0.06
RELAX2, FEED2 = 0.9, 0.025
STEP_PHASE = 0.7
IMPEDANCE = 0.35

STEPS = 4
NZ, CY, CX = 16, 128, 128
TILES = 512
SRCS = 256
PAD = 16
ROWS = PAD + CY + 16
CHUNK = 32
NG = 4
GZ = NZ // NG
PB = 4
XOUT = 4
LOW_X, HIGH_X, LOW_Y, HIGH_Y = 0, 1, 2, 3


def split2(value):
    high = value.astype(BF16)
    low = (value - high.astype(F32)).astype(BF16)
    return high, low


def split3(value):
    high = value.astype(BF16)
    rest = value - high.astype(F32)
    mid = rest.astype(BF16)
    low = (rest - mid.astype(F32)).astype(BF16)
    return high, mid, low


def dot(a, b):
    return lax.dot_general(a, b, (((1,), (0,)), ((), ())), preferred_element_type=F32)


def dot_nt(a, b):
    return lax.dot_general(a, b, (((1,), (1,)), ((), ())), preferred_element_type=F32)


def sincos_turns(turns):
    f = turns - jnp.floor(turns + 0.5)
    quad = jnp.floor(f * 4.0 + 0.5)
    x = (f - quad * 0.25) * (2.0 * math.pi)
    x2 = x * x
    s = x * (1.0 + x2 * (-1.0 / 6 + x2 * (1.0 / 120 + x2 * (-1.0 / 5040 + x2 * (1.0 / 362880)))))
    c = 1.0 + x2 * (-0.5 + x2 * (1.0 / 24 + x2 * (-1.0 / 720 + x2 * (1.0 / 40320))))
    swap = jnp.abs(quad) == 1.0
    a = jnp.where(swap, s, c)
    b = jnp.where(swap, c, s)
    cos_sign = jnp.where((quad == 0.0) | (quad == -1.0), 1.0, -1.0)
    sin_sign = jnp.where((quad == 0.0) | (quad == 1.0), 1.0, -1.0)
    return a * cos_sign, b * sin_sign


def pack_rows(read, group):
    packed = jnp.zeros((8, 128), F32)
    for block in range(16):
        rolled = pltpu.roll(read(block), (8 * block + 3) % 128, 1)
        packed = jnp.where(group == block, rolled, packed)
    return packed


def kernel(
    nx,
    ny,
    p_in,
    vx_in,
    vy_in,
    vz_in,
    m1_in,
    m2_in,
    de_in,
    cs_in,
    row_s,
    row_v,
    own_v,
    cell_v,
    wave_v,
    thi,
    tlo,
    wp,
    wv,
    p_out,
    VX,
    vy_out,
    vz_out,
    M1,
    M2,
    ff_out,
    P_,
    VY,
    VZ,
    B,
    MOD,
    CS,
    SRC,
    PO,
    PH,
    XO,
    XM,
    XH,
    TAB,
    HOT,
    HP,
    HV,
    G,
    RA,
    RC,
    ld_sem,
    st_sem,
    snd,
    rcv,
    snd0,
    rcv0,
    sa,
    ra,
    sc,
    rc,
):
    gx = lax.axis_index("gx")
    gy = lax.axis_index("gy")
    devices = nx * ny
    period = 2 * WAVELEN * max(ANG, devices)
    inner = nx // XOUT
    outer = ny * XOUT
    xo, xi = gx // inner, gx % inner
    has = [gx > 0, gx < nx - 1, gy > 0, gy < ny - 1]
    peer = [{"gx": gx - 1}, {"gx": gx + 1}, {"gy": gy - 1}, {"gy": gy + 1}]
    offsets = [(a, b) for a in range(ny) for b in range(XOUT)][1:]
    peers_a = [{"gx": (xo + b) % XOUT * inner + xi, "gy": (gy + a) % ny} for a, b in offsets]
    peers_c = [{"gx": xo * inner + (xi + k) % inner} for k in range(1, inner)]

    dst = [
        P_.at[0, pl.ds(1, NZ), pl.ds(PAD, CY), :],
        VX,
        VY.at[:, pl.ds(PAD, CY), :],
        VZ.at[0, pl.ds(2, NZ)],
        M1,
        M2,
        B.at[:, pl.ds(PAD, CY), :],
        CS,
    ]
    src = [p_in, vx_in, vy_in, vz_in, m1_in, m2_in, de_in, cs_in]
    loads = [pltpu.make_async_copy(src[i], dst[i], ld_sem.at[i]) for i in range(8)]
    for i in (0, 1, 6, 7, 2, 3, 4, 5):
        loads[i].start()

    barrier = pltpu.get_barrier_semaphore()
    for d in range(4):

        @pl.when(has[d])
        def _():
            pl.semaphore_signal(barrier, inc=1, device_id=peer[d], device_id_type=MESH)

    for target in peers_a + peers_c:
        pl.semaphore_signal(barrier, inc=1, device_id=target, device_id_type=MESH)
    fixed = len(peers_a) + len(peers_c)
    lane = lax.broadcasted_iota(jnp.int32, (8, 128), 1)
    group = lane >> 3
    from_low = (lane & 7) < 3

    def rim_copy(s, g, d):
        z0 = g * GZ
        if d in (LOW_X, HIGH_X):
            source = PO.at[s, pl.ds(z0, GZ)]
            target = PH.at[s, HIGH_X if d == LOW_X else LOW_X, pl.ds(z0, GZ)]
        else:
            y_from, y_to = (PAD, PAD + CY) if d == LOW_Y else (PAD + CY - 8, PAD - 8)
            source = P_.at[s, pl.ds(z0 + 1, GZ), pl.ds(y_from, 8), :]
            target = P_.at[s, pl.ds(z0 + 1, GZ), pl.ds(y_to, 8), :]
        back = {LOW_X: HIGH_X, HIGH_X: LOW_X, LOW_Y: HIGH_Y, HIGH_Y: LOW_Y}[d]
        return pltpu.make_async_remote_copy(
            src_ref=source,
            dst_ref=target,
            send_sem=snd.at[s, g, d],
            recv_sem=rcv.at[s, g, back],
            device_id=peer[d],
            device_id_type=MESH,
        )

    def send_rims(s, g):
        for d in range(4):

            @pl.when(has[d])
            def _():
                rim_copy(s, g, d).start()

    def wait_rims(s, g):
        for d in range(4):

            @pl.when(has[d])
            def _():
                back = {LOW_X: HIGH_X, HIGH_X: LOW_X, LOW_Y: HIGH_Y, HIGH_Y: LOW_Y}[d]
                rim_copy(s, g, back).wait_recv()

    def first_copies(d):
        back = {LOW_X: HIGH_X, HIGH_X: LOW_X, LOW_Y: HIGH_Y, HIGH_Y: LOW_Y}[d]
        if d in (LOW_X, HIGH_X):
            pairs = [(XO, XH.at[back])]
        else:
            y_from, y_to = (0, PAD + CY) if d == LOW_Y else (CY - 8, PAD - 8)
            pairs = [
                (vy_in.at[:, pl.ds(y_from, 8), :], VY.at[:, pl.ds(y_to, 8), :]),
                (de_in.at[:, pl.ds(y_from, 8), :], B.at[:, pl.ds(y_to, 8), :]),
            ]
        return [
            pltpu.make_async_remote_copy(
                src_ref=a,
                dst_ref=b,
                send_sem=snd0.at[d, i],
                recv_sem=rcv0.at[back, i],
                device_id=peer[d],
                device_id_type=MESH,
            )
            for i, (a, b) in enumerate(pairs)
        ]

    plane = jnp.zeros((CY, CX), F32)
    for s in range(STEPS):
        for z in (0, NZ + 1, NZ + 2):
            P_[s, z, PAD : PAD + CY, :] = plane
        for z in (0, 1, NZ + 2):
            VZ[s + 1, z] = plane
    rim = jnp.zeros((NZ, 8, 128), F32)
    for d in (LOW_X, HIGH_X):

        @pl.when(jnp.logical_not(has[d]))
        def _():
            for s in range(STEPS):
                PH[s, d] = rim
            XH[d, 0] = rim
            XH[d, 1] = rim + 1.0

    for d, y0 in ((LOW_Y, PAD - 8), (HIGH_Y, PAD + CY)):

        @pl.when(jnp.logical_not(has[d]))
        def _():
            for s in range(STEPS):
                P_[s, 1 : NZ + 1, y0 : y0 + 8, :] = rim
            VY[:, y0 : y0 + 8, :] = rim

    scale = 2.0 * math.pi / period
    magnitude = 2.0 * math.pi / WAVELEN
    angle = lax.broadcasted_iota(jnp.int32, (128, ANG), 1)
    wave_x = (2 * angle + 1 - ANG).astype(F32)
    x_turn = wave_x * (gx * CX).astype(F32)
    kx2 = (scale * wave_x) * (scale * wave_x)
    for k in range(TILES // 128):
        own = jnp.broadcast_to(own_v[:, k * 128 : (k + 1) * 128].astype(F32), (128, 128)).T
        row = jnp.broadcast_to(row_v[:, k * 128 : (k + 1) * 128].astype(F32), (128, 128)).T
        layer = jnp.floor(row * (1.0 / CY))
        tile_y = row - layer * CY + (gy * CY).astype(F32)
        wave_y = 2.0 * own + (1.0 - devices)
        ky = scale * wave_y
        wave_z = jnp.sqrt(magnitude * magnitude - kx2 - ky * ky)
        whole = (x_turn + wave_y * tile_y) * (1.0 / period)
        turns = (whole - jnp.floor(whole)) + wave_z * layer * (1.0 / (2.0 * math.pi))
        cosine, sine = sincos_turns(turns)
        TAB[0, k * 128 : (k + 1) * 128, :] = cosine
        TAB[1, k * 128 : (k + 1) * 128, :] = sine
        TAB[2, k * 128 : (k + 1) * 128, :] = wave_z * (1.0 / magnitude)

    loads[0].wait()

    def pack_first(z, carry):
        PO[0, z] = pack_rows(lambda k: P_[0, z + 1, PAD + 8 * k : PAD + 8 * k + 8, :], group)
        return carry

    lax.fori_loop(0, NZ, pack_first, 0)
    loads[1].wait()
    loads[6].wait()

    def pack_others(z, carry):
        XO[0, z] = pack_rows(lambda k: VX[z, 8 * k : 8 * k + 8, :], group)
        XO[1, z] = pack_rows(lambda k: B[z, PAD + 8 * k : PAD + 8 * k + 8, :], group)
        return carry

    lax.fori_loop(0, NZ, pack_others, 0)

    neighbours = sum(jnp.where(flag, 1, 0) for flag in has)
    pl.semaphore_wait(barrier, fixed + neighbours)
    for d in range(4):

        @pl.when(has[d])
        def _():
            for copy in first_copies(d):
                copy.start()

    for g in range(NG):
        send_rims(0, g)

    cells = cell_v[...]
    src_row = cells >> 7
    src_lane = cells & 127
    lane_hot = lax.broadcasted_iota(jnp.int32, (CX, SRCS), 0) == src_lane
    parts = []
    for s in range(STEPS):
        parts.append(split3(jnp.where(lane_hot, wave_v[s : s + 1, :], 0.0)))
    right = [jnp.concatenate([parts[s][i] for s in range(STEPS)], axis=0) for i in range(3)]
    for i in range(3):
        HOT[i] = right[i]

    def sources(z, carry):
        rows = lax.broadcasted_iota(jnp.int32, (CY, SRCS), 0) + z * CY
        hot = jnp.where(rows == src_row, 1.0, 0.0).astype(BF16)
        total = dot_nt(hot, HOT[0]) + dot_nt(hot, HOT[1]) + dot_nt(hot, HOT[2])
        for s in range(STEPS):
            SRC[s, z] = total[:, s * CX : (s + 1) * CX]
        return carry

    lax.fori_loop(0, NZ, sources, 0)

    for i in (7, 2, 3, 4, 5):
        loads[i].wait()
    for d in range(4):

        @pl.when(has[d])
        def _():
            back = {LOW_X: HIGH_X, HIGH_X: LOW_X, LOW_Y: HIGH_Y, HIGH_Y: LOW_Y}[d]
            for copy in first_copies(back):
                copy.wait_recv()

    low_ok = jnp.where(has[LOW_X], UNIT, 0.0)
    high_ok = jnp.where(has[HIGH_X], UNIT, 0.0)

    def material(z, carry):
        for y0 in range(0, CY, CHUNK):
            rho = B[z, PAD + y0 : PAD + y0 + CHUNK, :]
            speed = CS[z, y0 : y0 + CHUNK, :]
            MOD[z, y0 : y0 + CHUNK, :] = rho * speed * speed
            B[z, PAD + y0 : PAD + y0 + CHUNK, :] = UNIT / rho
        XM[0, z] = XO[0, z]
        XM[1, z] = UNIT / XO[1, z]
        XO[0, z] = jnp.where(from_low, XH[LOW_X, 0, z], XH[HIGH_X, 0, z])
        XO[1, z] = jnp.where(
            from_low, low_ok / XH[LOW_X, 1, z], high_ok / XH[HIGH_X, 1, z]
        )
        return carry

    for d in (LOW_X, HIGH_X):

        @pl.when(has[d])
        def _():
            for copy in first_copies(d):
                copy.wait_send()

    lax.fori_loop(0, NZ, material, 0)
    for d, y0 in ((LOW_Y, PAD - 8), (HIGH_Y, PAD + CY)):

        @pl.when(has[d])
        def _():
            B[:, y0 : y0 + 8, :] = UNIT / B[:, y0 : y0 + 8, :]

        @pl.when(jnp.logical_not(has[d]))
        def _():
            B[:, y0 : y0 + 8, :] = rim

    def corrected(change, first, second, weights):
        high = change.astype(BF16).astype(F32)
        rest = change - high
        mid = rest.astype(BF16).astype(F32)
        low = (rest - mid).astype(BF16).astype(F32)
        terms = jnp.where(first, high, jnp.where(second, pltpu.roll(mid, 3, 1), pltpu.roll(low, 126, 1)))
        left = [
            jnp.where(group == block, terms[8 * i : 8 * i + 8, :], 0.0)
            for i in range(PB)
            for block in range(CY // 8)
        ]
        fixed = dot(jnp.concatenate(left, axis=0).astype(BF16), weights)
        return fixed.reshape(PB, CY, CX)

    places = lax.broadcasted_iota(jnp.int32, (8 * PB, 128), 1) & 7
    lows = places < 3

    def rims(s, k):
        zs = pl.ds(k * PB, PB)

        def flat(v):
            return v.reshape(8 * PB, 128)

        near = jnp.where(lows, flat(PH[s, LOW_X, zs]), flat(PH[s, HIGH_X, zs]))
        mine = flat(PO[s, zs])
        low = jnp.where(lows, near, mine)
        high = jnp.where(lows, mine, near)

        def along(v):
            return NEAR * (pltpu.roll(v, 127, 1) - v) - (pltpu.roll(v, 126, 1) - pltpu.roll(v, 1, 1))

        along_low, along_high = along(low), along(high)
        theirs = flat(XO[0, zs]) - flat(XO[1, zs]) * jnp.where(lows, along_low, along_high)
        own = flat(XM[0, zs]) - flat(XM[1, zs]) * jnp.where(lows, along_high, along_low)
        XO[0, zs] = theirs.reshape(PB, 8, 128)
        XM[0, zs] = own.reshape(PB, 8, 128)
        HP[...] = corrected(near - mine, (places >= 2) & (places <= 4), places >= 5, wp[...])
        HV[k % 2] = corrected(theirs - own, (places >= 1) & (places <= 3), places >= 4, wv[...])

    def velocities(s, k):
        z = k * PB

        def at(dz, y0, y1):
            return P_[s, pl.ds(z + 1 + dz, PB), y0:y1, :]

        zs = pl.ds(z, PB)
        r, e = PAD, PAD + CY
        p = at(0, r, e)
        b = B[zs, r:e, :]
        fz = NEAR * (at(1, r, e) - p) - (at(2, r, e) - at(-1, r, e))
        new_z = VZ[s, pl.ds(z + 2, PB)] - b * fz
        fy = NEAR * (at(0, r + 1, e + 1) - p) - (at(0, r + 2, e + 2) - at(0, r - 1, e - 1))
        new_y = VY[zs, r:e, :] - b * fy
        fx = NEAR * (pltpu.roll(p, 127, 2) - p) - (pltpu.roll(p, 126, 2) - pltpu.roll(p, 1, 2))
        new_x = VX[zs] - b * (fx + HP[...])
        outside = []
        for y0 in (PAD - 8, PAD + CY):
            y1 = y0 + 8
            f = NEAR * (at(0, y0 + 1, y1 + 1) - at(0, y0, y1)) - (
                at(0, y0 + 2, y1 + 2) - at(0, y0 - 1, y1 - 1)
            )
            outside.append((y0, VY[zs, y0:y1, :] - B[zs, y0:y1, :] * f))
        VZ[s + 1, pl.ds(z + 2, PB)] = new_z
        VY[zs, r:e, :] = new_y
        VX[zs] = new_x
        for y0, value in outside:
            VY[zs, y0 : y0 + 8, :] = value

    def pressures(s, k):
        z = k * PB
        zs = pl.ds(z, PB)
        r, e = PAD, PAD + CY
        v = VX[zs]
        div = NEAR * (v - pltpu.roll(v, 1, 2)) - (pltpu.roll(v, 127, 2) - pltpu.roll(v, 2, 2))
        div = div + HV[k % 2]
        div = div + (
            NEAR * (VY[zs, r:e, :] - VY[zs, r - 1 : e - 1, :])
            - (VY[zs, r + 1 : e + 1, :] - VY[zs, r - 2 : e - 2, :])
        )

        def at(dz):
            return VZ[s + 1, pl.ds(z + 2 + dz, PB)]

        div = div + (NEAR * (at(0) - at(-1)) - (at(1) - at(-2)))
        one = RELAX1 * M1[zs] + (FEED1 * UNIT) * div
        two = RELAX2 * M2[zs] + (FEED2 * UNIT) * div
        new = P_[s, pl.ds(z + 1, PB), r:e, :] - MOD[zs] * (UNIT * div - one - two) + SRC[s, zs]
        M1[zs] = one
        M2[zs] = two
        P_[s + 1, pl.ds(z + 1, PB), r:e, :] = new
        for i in range(PB):
            PO[s + 1, z + i] = pack_rows(lambda q: new[i, 8 * q : 8 * q + 8, :], group)

    def stores(g):
        zs = pl.ds(g * GZ, GZ)
        pairs = [
            (P_.at[STEPS, pl.ds(g * GZ + 1, GZ), pl.ds(PAD, CY), :], p_out.at[zs]),
            (VY.at[zs, pl.ds(PAD, CY), :], vy_out.at[zs]),
            (VZ.at[STEPS, pl.ds(g * GZ + 2, GZ)], vz_out.at[zs]),
        ]
        return [pltpu.make_async_copy(a, b, st_sem.at[g, i]) for i, (a, b) in enumerate(pairs)]

    def step(s, carry):
        def planes(k, inner_carry):
            @pl.when(k < NZ // PB)
            def _():
                @pl.when(k % (GZ // PB) == 0)
                def _():
                    wait_rims(s, k // (GZ // PB))

                rims(s, k)
                velocities(s, k)

            @pl.when(k > 0)
            def _():
                pressures(s, k - 1)

                @pl.when(k % (GZ // PB) == 0)
                def _():
                    g = k // (GZ // PB) - 1

                    @pl.when(s < STEPS - 1)
                    def _():
                        send_rims(s + 1, g)

                    @pl.when(s == STEPS - 1)
                    def _():
                        for copy in stores(g):
                            copy.start()

            return inner_carry

        return lax.fori_loop(0, NZ // PB + 1, planes, carry)

    lax.fori_loop(0, STEPS, step, 0)

    def gather(t, carry):
        r = row_s[t]
        z = r >> 7
        y = r & 127
        for s in range(STEPS):
            G[s, pl.ds(t, 1), :] = P_[s + 1, z + 1, pl.ds(y + PAD, 1), :]
            G[STEPS + s, pl.ds(t, 1), :] = VZ[s + 1, z + 2, pl.ds(y, 1), :]
        return carry

    lax.fori_loop(0, TILES, gather, 0, unroll=8)

    weights = [(math.cos(STEP_PHASE * (s + 1)), math.sin(STEP_PHASE * (s + 1))) for s in range(STEPS)]
    own_row = own_v[...]
    order = (own_row % ny) * nx + own_row // ny
    hot = jnp.where(
        lax.broadcasted_iota(jnp.int32, (devices, TILES), 0) == order, 1.0, 0.0
    ).astype(BF16)
    total = jnp.zeros((devices, 2 * ANG), F32)
    for k in range(TILES // 128):
        t0, t1 = k * 128, (k + 1) * 128

        def mixed(base):
            fields = [G[base + s, t0:t1, :] for s in range(STEPS)]
            real = sum(weights[s][0] * fields[s] for s in range(STEPS))
            imag = sum(weights[s][1] * fields[s] for s in range(STEPS))
            high, low = split2(jnp.concatenate([real, imag], axis=1))
            return dot(high, thi[...]) + dot(low, thi[...]) + dot(high, tlo[...])

        press = mixed(0)
        flow = mixed(STEPS)
        cosine, sine, lift = TAB[0, t0:t1, :], TAB[1, t0:t1, :], TAB[2, t0:t1, :]
        real = lift * press[:, :ANG] + IMPEDANCE * flow[:, :ANG]
        imag = lift * press[:, ANG:] + IMPEDANCE * flow[:, ANG:]
        both = jnp.concatenate([cosine * real + sine * imag, cosine * imag - sine * real], axis=1)
        high, low = split2(both)
        total = total + (dot(hot[:, t0:t1], high) + dot(hot[:, t0:t1], low))
    for j in range(outer):
        RA[outer + j] = total[j * inner : (j + 1) * inner, :]

    def exchange(targets, source_of, slots, send, recv):
        copies = []
        for k, target in enumerate(targets):
            copy = pltpu.make_async_remote_copy(
                src_ref=source_of(k + 1),
                dst_ref=slots.at[k + 1],
                send_sem=send.at[k],
                recv_sem=recv.at[k],
                device_id=target,
                device_id_type=MESH,
            )
            copy.start()
            copies.append(copy)
        return copies

    def block_of(a, b):
        return (gy + a) % ny * XOUT + (xo + b) % XOUT

    copies = exchange(peers_a, lambda k: RA.at[outer + block_of(*offsets[k - 1])], RA, sa, ra)
    part = RA[outer + block_of(0, 0)]
    for k, copy in enumerate(copies):
        copy.wait()
        part = part + RA[k + 1]
    RC[0] = part
    copies = exchange(peers_c, lambda k: RC.at[0], RC, sc, rc)
    for k, copy in enumerate(copies):
        copy.wait()
        part = part + RC[k + 1]
    norm = 1.0 / math.sqrt(TILES * CX)
    keep = lax.broadcasted_iota(jnp.int32, (inner, 2 * ANG), 0) == xi
    final = jnp.sum(jnp.where(keep, part, 0.0), axis=0, keepdims=True) * norm
    ff_out[0:1, :] = final[:, :ANG]
    ff_out[1:2, :] = final[:, ANG:]

    def drain(i, carry):
        s, g = i // NG, i % NG
        for d in range(4):

            @pl.when(has[d])
            def _():
                rim_copy(s, g, d).wait_send()

        return carry

    lax.fori_loop(0, STEPS * NG, drain, 0)
    for d in (LOW_Y, HIGH_Y):

        @pl.when(has[d])
        def _():
            for copy in first_copies(d):
                copy.wait_send()

    for g in range(NG):
        for copy in stores(g):
            copy.wait()


def tables():
    period = 4096
    wave = 2 * np.arange(ANG) + 1 - ANG
    phase = 2.0 * np.pi * ((np.arange(CX)[:, None] * wave[None, :]) % period) / period
    c, s = np.cos(phase), np.sin(phase)
    table = np.concatenate(
        [np.concatenate([c, -s], axis=1), np.concatenate([s, c], axis=1)], axis=0
    ).astype(np.float32)
    high = table.astype(jnp.bfloat16)
    low = (table - high.astype(np.float32)).astype(jnp.bfloat16)
    return high, low


def edge_weights():
    forward = np.zeros((8, CX), np.float32)
    for place in (0, 2, 5):
        forward[place, 0] = 1.0
    for place in (1, 3, 6):
        forward[place, CX - 1] = NEAR
        forward[place, CX - 2] = -1.0
    for place in (4, 7):
        forward[place, CX - 1] = -1.0
    backward = np.zeros((8, CX), np.float32)
    for place in (1, 4):
        backward[place, 0] = 1.0
    for place in (0, 2, 5):
        backward[place, 0] = -NEAR
        backward[place, 1] = 1.0
    for place in (3, 6):
        backward[place, CX - 1] = -1.0
    return [np.tile(w, (16, 1)).astype(jnp.bfloat16) for w in (forward, backward)]


def local(nx, ny, *args):
    fields = args[:8]
    tile_row, tile_owner, src_cell, src_wave = args[8:]
    rows = tile_row.reshape(TILES)
    high, low = tables()
    anywhere = pl.BlockSpec(memory_space=pl.ANY)
    vmem = pl.BlockSpec(memory_space=pltpu.VMEM)
    smem = pl.BlockSpec(memory_space=pltpu.SMEM)
    dma = pltpu.SemaphoreType.DMA
    inner = nx // XOUT
    outer = ny * XOUT
    return pl.pallas_call(
        functools.partial(kernel, nx, ny),
        out_shape=[pltpu.VMEM((NZ, CY, CX), F32)] * 6 + [jax.ShapeDtypeStruct((2, ANG), F32)],
        in_specs=[anywhere] * 8 + [smem] + [vmem] * 8,
        out_specs=[vmem] * 7,
        scratch_shapes=[
            pltpu.VMEM((STEPS + 1, NZ + 3, ROWS, CX), F32),
            pltpu.VMEM((NZ, ROWS, CX), F32),
            pltpu.VMEM((STEPS + 1, NZ + 3, CY, CX), F32),
            pltpu.VMEM((NZ, ROWS, CX), F32),
            pltpu.VMEM((NZ, CY, CX), F32),
            pltpu.VMEM((NZ, CY, CX), F32),
            pltpu.VMEM((STEPS, NZ, CY, CX), F32),
            pltpu.VMEM((STEPS + 1, NZ, 8, CX), F32),
            pltpu.VMEM((STEPS, 2, NZ, 8, CX), F32),
            pltpu.VMEM((2, NZ, 8, CX), F32),
            pltpu.VMEM((2, NZ, 8, CX), F32),
            pltpu.VMEM((2, 2, NZ, 8, CX), F32),
            pltpu.VMEM((3, TILES, ANG), F32),
            pltpu.VMEM((3, STEPS * CX, SRCS), BF16),
            pltpu.VMEM((PB, CY, CX), F32),
            pltpu.VMEM((2, PB, CY, CX), F32),
            pltpu.VMEM((2 * STEPS, TILES, CX), F32),
            pltpu.VMEM((2 * outer, inner, 2 * ANG), F32),
            pltpu.VMEM((inner, inner, 2 * ANG), F32),
            dma((8,)),
            dma((NG, 3)),
            dma((STEPS, NG, 4)),
            dma((STEPS, NG, 4)),
            dma((4, 2)),
            dma((4, 2)),
            dma((outer - 1,)),
            dma((outer - 1,)),
            dma((inner - 1,)),
            dma((inner - 1,)),
        ],
        compiler_params=pltpu.CompilerParams(
            collective_id=0, has_side_effects=True, vmem_limit_bytes=56 * 1024 * 1024
        ),
    )(
        *fields,
        rows,
        rows.reshape(1, TILES),
        tile_owner.reshape(1, TILES),
        src_cell.reshape(1, SRCS),
        src_wave.reshape(STEPS, SRCS),
        high,
        low,
        *edge_weights(),
    )


def solution(mesh):
    field = P(None, "gy", "gx")
    return jax.shard_map(
        functools.partial(local, mesh.shape["gx"], mesh.shape["gy"]),
        mesh=mesh,
        in_specs=(field,) * 8
        + (
            P("gy", "gx", None),
            P("gy", "gx", None, None),
            P("gy", "gx", None),
            P("gy", "gx", None, None),
        ),
        out_specs=(field,) * 6 + (P(None, ("gx", "gy")),),
        check_vma=False,
    )
```

```python
import functools
import math

import jax
import jax.numpy as jnp
import numpy as np
from jax import lax
from jax.experimental import pallas as pl
from jax.experimental.pallas import tpu as pltpu
from jax.sharding import PartitionSpec as P

MESH = pl.DeviceIdType.MESH
F32 = jnp.float32
BF16 = jnp.bfloat16

ANG = 128
WAVELEN = 16
UNIT = 1.0 / 24.0
NEAR = 27.0
RELAX1, FEED1 = 0.6, 0.06
RELAX2, FEED2 = 0.9, 0.025
STEP_PHASE = 0.7
IMPEDANCE = 0.35

STEPS = 4
NZ, CY, CX = 16, 128, 128
TILES = 512
SRCS = 256
PAD = 16
ROWS = PAD + CY + 16
CHUNK = 32
NG = 4
GZ = NZ // NG
PB = 4
XOUT = 4
LOW_X, HIGH_X, LOW_Y, HIGH_Y = 0, 1, 2, 3


def split2(value):
    high = value.astype(BF16)
    low = (value - high.astype(F32)).astype(BF16)
    return high, low


def split3(value):
    high = value.astype(BF16)
    rest = value - high.astype(F32)
    mid = rest.astype(BF16)
    low = (rest - mid.astype(F32)).astype(BF16)
    return high, mid, low


def dot(a, b):
    return lax.dot_general(a, b, (((1,), (0,)), ((), ())), preferred_element_type=F32)


def dot_nt(a, b):
    return lax.dot_general(a, b, (((1,), (1,)), ((), ())), preferred_element_type=F32)


def sincos_turns(turns):
    f = turns - jnp.floor(turns + 0.5)
    quad = jnp.floor(f * 4.0 + 0.5)
    x = (f - quad * 0.25) * (2.0 * math.pi)
    x2 = x * x
    s = x * (1.0 + x2 * (-1.0 / 6 + x2 * (1.0 / 120 + x2 * (-1.0 / 5040 + x2 * (1.0 / 362880)))))
    c = 1.0 + x2 * (-0.5 + x2 * (1.0 / 24 + x2 * (-1.0 / 720 + x2 * (1.0 / 40320))))
    swap = jnp.abs(quad) == 1.0
    a = jnp.where(swap, s, c)
    b = jnp.where(swap, c, s)
    cos_sign = jnp.where((quad == 0.0) | (quad == -1.0), 1.0, -1.0)
    sin_sign = jnp.where((quad == 0.0) | (quad == 1.0), 1.0, -1.0)
    return a * cos_sign, b * sin_sign


def pack_rows(read, group):
    packed = jnp.zeros((8, 128), F32)
    for block in range(16):
        rolled = pltpu.roll(read(block), (8 * block + 3) % 128, 1)
        packed = jnp.where(group == block, rolled, packed)
    return packed


def kernel(
    nx,
    ny,
    p_in,
    vx_in,
    vy_in,
    vz_in,
    m1_in,
    m2_in,
    de_in,
    cs_in,
    row_s,
    row_v,
    own_v,
    cell_v,
    wave_v,
    thi,
    tlo,
    wp,
    wv,
    p_out,
    VX,
    vy_out,
    vz_out,
    M1,
    M2,
    ff_out,
    P_,
    VY,
    VZ,
    B,
    MOD,
    CS,
    SRC,
    PO,
    PH,
    XO,
    XM,
    XH,
    TAB,
    HOT,
    HP,
    HV,
    G,
    RA,
    RC,
    ld_sem,
    st_sem,
    snd,
    rcv,
    snd0,
    rcv0,
    sa,
    ra,
    sc,
    rc,
):
    gx = lax.axis_index("gx")
    gy = lax.axis_index("gy")
    devices = nx * ny
    period = 2 * WAVELEN * max(ANG, devices)
    inner = nx // XOUT
    outer = ny * XOUT
    xo, xi = gx // inner, gx % inner
    has = [gx > 0, gx < nx - 1, gy > 0, gy < ny - 1]
    peer = [{"gx": gx - 1}, {"gx": gx + 1}, {"gy": gy - 1}, {"gy": gy + 1}]
    offsets = [(a, b) for a in range(ny) for b in range(XOUT)][1:]
    peers_a = [{"gx": (xo + b) % XOUT * inner + xi, "gy": (gy + a) % ny} for a, b in offsets]
    peers_c = [{"gx": xo * inner + (xi + k) % inner} for k in range(1, inner)]

    dst = [
        P_.at[0, pl.ds(1, NZ), pl.ds(PAD, CY), :],
        VX,
        VY.at[:, pl.ds(PAD, CY), :],
        VZ.at[0, pl.ds(2, NZ)],
        M1,
        M2,
        B.at[:, pl.ds(PAD, CY), :],
        CS,
    ]
    src = [p_in, vx_in, vy_in, vz_in, m1_in, m2_in, de_in, cs_in]
    loads = [pltpu.make_async_copy(src[i], dst[i], ld_sem.at[i]) for i in range(8)]
    for i in (0, 1, 6, 7, 2, 3, 4, 5):
        loads[i].start()

    barrier = pltpu.get_barrier_semaphore()
    for d in range(4):

        @pl.when(has[d])
        def _():
            pl.semaphore_signal(barrier, inc=1, device_id=peer[d], device_id_type=MESH)

    for target in peers_a + peers_c:
        pl.semaphore_signal(barrier, inc=1, device_id=target, device_id_type=MESH)
    fixed = len(peers_a) + len(peers_c)
    lane = lax.broadcasted_iota(jnp.int32, (8, 128), 1)
    group = lane >> 3
    from_low = (lane & 7) < 3

    def rim_copy(s, g, d):
        z0 = g * GZ
        if d in (LOW_X, HIGH_X):
            source = PO.at[s, pl.ds(z0, GZ)]
            target = PH.at[s, HIGH_X if d == LOW_X else LOW_X, pl.ds(z0, GZ)]
        else:
            y_from, y_to = (PAD, PAD + CY) if d == LOW_Y else (PAD + CY - 4, PAD - 4)
            source = P_.at[s, pl.ds(z0 + 1, GZ), pl.ds(y_from, 4), :]
            target = P_.at[s, pl.ds(z0 + 1, GZ), pl.ds(y_to, 4), :]
        back = {LOW_X: HIGH_X, HIGH_X: LOW_X, LOW_Y: HIGH_Y, HIGH_Y: LOW_Y}[d]
        return pltpu.make_async_remote_copy(
            src_ref=source,
            dst_ref=target,
            send_sem=snd.at[s, g, d],
            recv_sem=rcv.at[s, g, back],
            device_id=peer[d],
            device_id_type=MESH,
        )

    def send_rims(s, g):
        for d in range(4):

            @pl.when(has[d])
            def _():
                rim_copy(s, g, d).start()

    def wait_rims(s, g):
        for d in range(4):

            @pl.when(has[d])
            def _():
                back = {LOW_X: HIGH_X, HIGH_X: LOW_X, LOW_Y: HIGH_Y, HIGH_Y: LOW_Y}[d]
                rim_copy(s, g, back).wait_recv()

    def first_copies(d):
        back = {LOW_X: HIGH_X, HIGH_X: LOW_X, LOW_Y: HIGH_Y, HIGH_Y: LOW_Y}[d]
        if d in (LOW_X, HIGH_X):
            pairs = [(XO, XH.at[back])]
        else:
            y_from, y_to = (0, PAD + CY) if d == LOW_Y else (CY - 4, PAD - 4)
            pairs = [
                (vy_in.at[:, pl.ds(y_from, 4), :], VY.at[:, pl.ds(y_to, 4), :]),
                (de_in.at[:, pl.ds(y_from, 4), :], B.at[:, pl.ds(y_to, 4), :]),
            ]
        return [
            pltpu.make_async_remote_copy(
                src_ref=a,
                dst_ref=b,
                send_sem=snd0.at[d, i],
                recv_sem=rcv0.at[back, i],
                device_id=peer[d],
                device_id_type=MESH,
            )
            for i, (a, b) in enumerate(pairs)
        ]

    plane = jnp.zeros((CY, CX), F32)
    for s in range(STEPS):
        for z in (0, NZ + 1, NZ + 2):
            P_[s, z, PAD : PAD + CY, :] = plane
        for z in (0, 1, NZ + 2):
            VZ[s + 1, z] = plane
    rim = jnp.zeros((NZ, 8, 128), F32)
    for d in (LOW_X, HIGH_X):

        @pl.when(jnp.logical_not(has[d]))
        def _():
            for s in range(STEPS):
                PH[s, d] = rim
            XH[d, 0] = rim
            XH[d, 1] = rim + 1.0

    for d, y0 in ((LOW_Y, PAD - 8), (HIGH_Y, PAD + CY)):

        @pl.when(jnp.logical_not(has[d]))
        def _():
            for s in range(STEPS):
                P_[s, 1 : NZ + 1, y0 : y0 + 8, :] = rim
            VY[:, y0 : y0 + 8, :] = rim

    scale = 2.0 * math.pi / period
    magnitude = 2.0 * math.pi / WAVELEN
    angle = lax.broadcasted_iota(jnp.int32, (128, ANG), 1)
    wave_x = (2 * angle + 1 - ANG).astype(F32)
    x_turn = wave_x * (gx * CX).astype(F32)
    kx2 = (scale * wave_x) * (scale * wave_x)
    for k in range(TILES // 128):
        own = jnp.broadcast_to(own_v[:, k * 128 : (k + 1) * 128].astype(F32), (128, 128)).T
        row = jnp.broadcast_to(row_v[:, k * 128 : (k + 1) * 128].astype(F32), (128, 128)).T
        layer = jnp.floor(row * (1.0 / CY))
        tile_y = row - layer * CY + (gy * CY).astype(F32)
        wave_y = 2.0 * own + (1.0 - devices)
        ky = scale * wave_y
        wave_z = jnp.sqrt(magnitude * magnitude - kx2 - ky * ky)
        whole = (x_turn + wave_y * tile_y) * (1.0 / period)
        turns = (whole - jnp.floor(whole)) + wave_z * layer * (1.0 / (2.0 * math.pi))
        cosine, sine = sincos_turns(turns)
        TAB[0, k * 128 : (k + 1) * 128, :] = cosine
        TAB[1, k * 128 : (k + 1) * 128, :] = sine
        TAB[2, k * 128 : (k + 1) * 128, :] = wave_z * (1.0 / magnitude)

    loads[0].wait()

    def pack_first(z, carry):
        PO[0, z] = pack_rows(lambda k: P_[0, z + 1, PAD + 8 * k : PAD + 8 * k + 8, :], group)
        return carry

    lax.fori_loop(0, NZ, pack_first, 0)
    loads[1].wait()
    loads[6].wait()

    def pack_others(z, carry):
        XO[0, z] = pack_rows(lambda k: VX[z, 8 * k : 8 * k + 8, :], group)
        XO[1, z] = pack_rows(lambda k: B[z, PAD + 8 * k : PAD + 8 * k + 8, :], group)
        return carry

    lax.fori_loop(0, NZ, pack_others, 0)

    neighbours = sum(jnp.where(flag, 1, 0) for flag in has)
    pl.semaphore_wait(barrier, fixed + neighbours)
    for d in range(4):

        @pl.when(has[d])
        def _():
            for copy in first_copies(d):
                copy.start()

    for g in range(NG):
        send_rims(0, g)

    cells = cell_v[...]
    src_row = cells >> 7
    src_lane = cells & 127
    lane_hot = lax.broadcasted_iota(jnp.int32, (CX, SRCS), 0) == src_lane
    parts = []
    for s in range(STEPS):
        parts.append(split3(jnp.where(lane_hot, wave_v[s : s + 1, :], 0.0)))
    right = [jnp.concatenate([parts[s][i] for s in range(STEPS)], axis=0) for i in range(3)]
    for i in range(3):
        HOT[i] = right[i]

    def sources(z, carry):
        rows = lax.broadcasted_iota(jnp.int32, (CY, SRCS), 0) + z * CY
        hot = jnp.where(rows == src_row, 1.0, 0.0).astype(BF16)
        total = dot_nt(hot, HOT[0]) + dot_nt(hot, HOT[1]) + dot_nt(hot, HOT[2])
        for s in range(STEPS):
            SRC[s, z] = total[:, s * CX : (s + 1) * CX]
        return carry

    lax.fori_loop(0, NZ, sources, 0)

    for i in (7, 2, 3, 4, 5):
        loads[i].wait()
    for d in range(4):

        @pl.when(has[d])
        def _():
            back = {LOW_X: HIGH_X, HIGH_X: LOW_X, LOW_Y: HIGH_Y, HIGH_Y: LOW_Y}[d]
            for copy in first_copies(back):
                copy.wait_recv()

    low_ok = jnp.where(has[LOW_X], UNIT, 0.0)
    high_ok = jnp.where(has[HIGH_X], UNIT, 0.0)

    def material(z, carry):
        for y0 in range(0, CY, CHUNK):
            rho = B[z, PAD + y0 : PAD + y0 + CHUNK, :]
            speed = CS[z, y0 : y0 + CHUNK, :]
            MOD[z, y0 : y0 + CHUNK, :] = rho * speed * speed
            B[z, PAD + y0 : PAD + y0 + CHUNK, :] = UNIT / rho
        XM[0, z] = XO[0, z]
        XM[1, z] = UNIT / XO[1, z]
        XO[0, z] = jnp.where(from_low, XH[LOW_X, 0, z], XH[HIGH_X, 0, z])
        XO[1, z] = jnp.where(
            from_low, low_ok / XH[LOW_X, 1, z], high_ok / XH[HIGH_X, 1, z]
        )
        return carry

    for d in (LOW_X, HIGH_X):

        @pl.when(has[d])
        def _():
            for copy in first_copies(d):
                copy.wait_send()

    lax.fori_loop(0, NZ, material, 0)
    for d, y0 in ((LOW_Y, PAD - 8), (HIGH_Y, PAD + CY)):

        @pl.when(has[d])
        def _():
            B[:, y0 : y0 + 8, :] = UNIT / B[:, y0 : y0 + 8, :]

        @pl.when(jnp.logical_not(has[d]))
        def _():
            B[:, y0 : y0 + 8, :] = rim

    def corrected(change, first, second, weights):
        high = change.astype(BF16).astype(F32)
        rest = change - high
        mid = rest.astype(BF16).astype(F32)
        low = (rest - mid).astype(BF16).astype(F32)
        terms = jnp.where(first, high, jnp.where(second, pltpu.roll(mid, 3, 1), pltpu.roll(low, 126, 1)))
        left = [
            jnp.where(group == block, terms[8 * i : 8 * i + 8, :], 0.0)
            for i in range(PB)
            for block in range(CY // 8)
        ]
        fixed = dot(jnp.concatenate(left, axis=0).astype(BF16), weights)
        return fixed.reshape(PB, CY, CX)

    places = lax.broadcasted_iota(jnp.int32, (8 * PB, 128), 1) & 7
    lows = places < 3

    def rims(s, k):
        zs = pl.ds(k * PB, PB)

        def flat(v):
            return v.reshape(8 * PB, 128)

        near = jnp.where(lows, flat(PH[s, LOW_X, zs]), flat(PH[s, HIGH_X, zs]))
        mine = flat(PO[s, zs])
        low = jnp.where(lows, near, mine)
        high = jnp.where(lows, mine, near)

        def along(v):
            return NEAR * (pltpu.roll(v, 127, 1) - v) - (pltpu.roll(v, 126, 1) - pltpu.roll(v, 1, 1))

        along_low, along_high = along(low), along(high)
        theirs = flat(XO[0, zs]) - flat(XO[1, zs]) * jnp.where(lows, along_low, along_high)
        own = flat(XM[0, zs]) - flat(XM[1, zs]) * jnp.where(lows, along_high, along_low)
        XO[0, zs] = theirs.reshape(PB, 8, 128)
        XM[0, zs] = own.reshape(PB, 8, 128)
        HP[...] = corrected(near - mine, (places >= 2) & (places <= 4), places >= 5, wp[...])
        HV[k % 2] = corrected(theirs - own, (places >= 1) & (places <= 3), places >= 4, wv[...])

    def velocities(s, k):
        z = k * PB

        def at(dz, y0, y1):
            return P_[s, pl.ds(z + 1 + dz, PB), y0:y1, :]

        zs = pl.ds(z, PB)
        r, e = PAD, PAD + CY
        p = at(0, r, e)
        b = B[zs, r:e, :]
        fz = NEAR * (at(1, r, e) - p) - (at(2, r, e) - at(-1, r, e))
        new_z = VZ[s, pl.ds(z + 2, PB)] - b * fz
        fy = NEAR * (at(0, r + 1, e + 1) - p) - (at(0, r + 2, e + 2) - at(0, r - 1, e - 1))
        new_y = VY[zs, r:e, :] - b * fy
        fx = NEAR * (pltpu.roll(p, 127, 2) - p) - (pltpu.roll(p, 126, 2) - pltpu.roll(p, 1, 2))
        new_x = VX[zs] - b * (fx + HP[...])
        outside = []
        for y0 in (PAD - 8, PAD + CY):
            y1 = y0 + 8
            f = NEAR * (at(0, y0 + 1, y1 + 1) - at(0, y0, y1)) - (
                at(0, y0 + 2, y1 + 2) - at(0, y0 - 1, y1 - 1)
            )
            outside.append((y0, VY[zs, y0:y1, :] - B[zs, y0:y1, :] * f))
        VZ[s + 1, pl.ds(z + 2, PB)] = new_z
        VY[zs, r:e, :] = new_y
        VX[zs] = new_x
        for y0, value in outside:
            VY[zs, y0 : y0 + 8, :] = value

    def pressures(s, k):
        z = k * PB
        zs = pl.ds(z, PB)
        r, e = PAD, PAD + CY
        v = VX[zs]
        div = NEAR * (v - pltpu.roll(v, 1, 2)) - (pltpu.roll(v, 127, 2) - pltpu.roll(v, 2, 2))
        div = div + HV[k % 2]
        div = div + (
            NEAR * (VY[zs, r:e, :] - VY[zs, r - 1 : e - 1, :])
            - (VY[zs, r + 1 : e + 1, :] - VY[zs, r - 2 : e - 2, :])
        )

        def at(dz):
            return VZ[s + 1, pl.ds(z + 2 + dz, PB)]

        div = div + (NEAR * (at(0) - at(-1)) - (at(1) - at(-2)))
        one = RELAX1 * M1[zs] + (FEED1 * UNIT) * div
        two = RELAX2 * M2[zs] + (FEED2 * UNIT) * div
        new = P_[s, pl.ds(z + 1, PB), r:e, :] - MOD[zs] * (UNIT * div - one - two) + SRC[s, zs]
        M1[zs] = one
        M2[zs] = two
        P_[s + 1, pl.ds(z + 1, PB), r:e, :] = new
        for i in range(PB):
            PO[s + 1, z + i] = pack_rows(lambda q: new[i, 8 * q : 8 * q + 8, :], group)

    def stores(g):
        zs = pl.ds(g * GZ, GZ)
        pairs = [
            (P_.at[STEPS, pl.ds(g * GZ + 1, GZ), pl.ds(PAD, CY), :], p_out.at[zs]),
            (VY.at[zs, pl.ds(PAD, CY), :], vy_out.at[zs]),
            (VZ.at[STEPS, pl.ds(g * GZ + 2, GZ)], vz_out.at[zs]),
        ]
        return [pltpu.make_async_copy(a, b, st_sem.at[g, i]) for i, (a, b) in enumerate(pairs)]

    def step(s, carry):
        def planes(k, inner_carry):
            @pl.when(k < NZ // PB)
            def _():
                @pl.when(k % (GZ // PB) == 0)
                def _():
                    wait_rims(s, k // (GZ // PB))

                rims(s, k)
                velocities(s, k)

            @pl.when(k > 0)
            def _():
                pressures(s, k - 1)

                @pl.when(k % (GZ // PB) == 0)
                def _():
                    g = k // (GZ // PB) - 1

                    @pl.when(s < STEPS - 1)
                    def _():
                        send_rims(s + 1, g)

                    @pl.when(s == STEPS - 1)
                    def _():
                        for copy in stores(g):
                            copy.start()

            return inner_carry

        return lax.fori_loop(0, NZ // PB + 1, planes, carry)

    lax.fori_loop(0, STEPS, step, 0)

    def gather(t, carry):
        r = row_s[t]
        z = r >> 7
        y = r & 127
        for s in range(STEPS):
            G[s, pl.ds(t, 1), :] = P_[s + 1, z + 1, pl.ds(y + PAD, 1), :]
            G[STEPS + s, pl.ds(t, 1), :] = VZ[s + 1, z + 2, pl.ds(y, 1), :]
        return carry

    lax.fori_loop(0, TILES, gather, 0, unroll=32)

    weights = [(math.cos(STEP_PHASE * (s + 1)), math.sin(STEP_PHASE * (s + 1))) for s in range(STEPS)]
    own_row = own_v[...]
    order = (own_row % ny) * nx + own_row // ny
    hot = jnp.where(
        lax.broadcasted_iota(jnp.int32, (devices, TILES), 0) == order, 1.0, 0.0
    ).astype(BF16)
    total = jnp.zeros((devices, 2 * ANG), F32)
    for k in range(TILES // 128):
        t0, t1 = k * 128, (k + 1) * 128

        def mixed(base):
            fields = [G[base + s, t0:t1, :] for s in range(STEPS)]
            real = sum(weights[s][0] * fields[s] for s in range(STEPS))
            imag = sum(weights[s][1] * fields[s] for s in range(STEPS))
            high, low = split2(jnp.concatenate([real, imag], axis=1))
            return dot(high, thi[...]) + dot(low, thi[...]) + dot(high, tlo[...])

        press = mixed(0)
        flow = mixed(STEPS)
        cosine, sine, lift = TAB[0, t0:t1, :], TAB[1, t0:t1, :], TAB[2, t0:t1, :]
        real = lift * press[:, :ANG] + IMPEDANCE * flow[:, :ANG]
        imag = lift * press[:, ANG:] + IMPEDANCE * flow[:, ANG:]
        both = jnp.concatenate([cosine * real + sine * imag, cosine * imag - sine * real], axis=1)
        high, low = split2(both)
        total = total + (dot(hot[:, t0:t1], high) + dot(hot[:, t0:t1], low))
    for j in range(outer):
        RA[outer + j] = total[j * inner : (j + 1) * inner, :]

    def exchange(targets, source_of, slots, send, recv):
        copies = []
        for k, target in enumerate(targets):
            copy = pltpu.make_async_remote_copy(
                src_ref=source_of(k + 1),
                dst_ref=slots.at[k + 1],
                send_sem=send.at[k],
                recv_sem=recv.at[k],
                device_id=target,
                device_id_type=MESH,
            )
            copy.start()
            copies.append(copy)
        return copies

    def block_of(a, b):
        return (gy + a) % ny * XOUT + (xo + b) % XOUT

    copies = exchange(peers_a, lambda k: RA.at[outer + block_of(*offsets[k - 1])], RA, sa, ra)
    part = RA[outer + block_of(0, 0)]
    for k, copy in enumerate(copies):
        copy.wait()
        part = part + RA[k + 1]
    RC[0] = part
    copies = exchange(peers_c, lambda k: RC.at[0], RC, sc, rc)
    for k, copy in enumerate(copies):
        copy.wait()
        part = part + RC[k + 1]
    norm = 1.0 / math.sqrt(TILES * CX)
    keep = lax.broadcasted_iota(jnp.int32, (inner, 2 * ANG), 0) == xi
    final = jnp.sum(jnp.where(keep, part, 0.0), axis=0, keepdims=True) * norm
    ff_out[0:1, :] = final[:, :ANG]
    ff_out[1:2, :] = final[:, ANG:]

    def drain(i, carry):
        s, g = i // NG, i % NG
        for d in range(4):

            @pl.when(has[d])
            def _():
                rim_copy(s, g, d).wait_send()

        return carry

    lax.fori_loop(0, STEPS * NG, drain, 0)
    for d in (LOW_Y, HIGH_Y):

        @pl.when(has[d])
        def _():
            for copy in first_copies(d):
                copy.wait_send()

    for g in range(NG):
        for copy in stores(g):
            copy.wait()


def tables():
    period = 4096
    wave = 2 * np.arange(ANG) + 1 - ANG
    phase = 2.0 * np.pi * ((np.arange(CX)[:, None] * wave[None, :]) % period) / period
    c, s = np.cos(phase), np.sin(phase)
    table = np.concatenate(
        [np.concatenate([c, -s], axis=1), np.concatenate([s, c], axis=1)], axis=0
    ).astype(np.float32)
    high = table.astype(jnp.bfloat16)
    low = (table - high.astype(np.float32)).astype(jnp.bfloat16)
    return high, low


def edge_weights():
    forward = np.zeros((8, CX), np.float32)
    for place in (0, 2, 5):
        forward[place, 0] = 1.0
    for place in (1, 3, 6):
        forward[place, CX - 1] = NEAR
        forward[place, CX - 2] = -1.0
    for place in (4, 7):
        forward[place, CX - 1] = -1.0
    backward = np.zeros((8, CX), np.float32)
    for place in (1, 4):
        backward[place, 0] = 1.0
    for place in (0, 2, 5):
        backward[place, 0] = -NEAR
        backward[place, 1] = 1.0
    for place in (3, 6):
        backward[place, CX - 1] = -1.0
    return [np.tile(w, (16, 1)).astype(jnp.bfloat16) for w in (forward, backward)]


def local(nx, ny, *args):
    fields = args[:8]
    tile_row, tile_owner, src_cell, src_wave = args[8:]
    rows = tile_row.reshape(TILES)
    high, low = tables()
    anywhere = pl.BlockSpec(memory_space=pl.ANY)
    vmem = pl.BlockSpec(memory_space=pltpu.VMEM)
    smem = pl.BlockSpec(memory_space=pltpu.SMEM)
    dma = pltpu.SemaphoreType.DMA
    inner = nx // XOUT
    outer = ny * XOUT
    return pl.pallas_call(
        functools.partial(kernel, nx, ny),
        out_shape=[pltpu.VMEM((NZ, CY, CX), F32)] * 6 + [jax.ShapeDtypeStruct((2, ANG), F32)],
        in_specs=[anywhere] * 8 + [smem] + [vmem] * 8,
        out_specs=[vmem] * 7,
        scratch_shapes=[
            pltpu.VMEM((STEPS + 1, NZ + 3, ROWS, CX), F32),
            pltpu.VMEM((NZ, ROWS, CX), F32),
            pltpu.VMEM((STEPS + 1, NZ + 3, CY, CX), F32),
            pltpu.VMEM((NZ, ROWS, CX), F32),
            pltpu.VMEM((NZ, CY, CX), F32),
            pltpu.VMEM((NZ, CY, CX), F32),
            pltpu.VMEM((STEPS, NZ, CY, CX), F32),
            pltpu.VMEM((STEPS + 1, NZ, 8, CX), F32),
            pltpu.VMEM((STEPS, 2, NZ, 8, CX), F32),
            pltpu.VMEM((2, NZ, 8, CX), F32),
            pltpu.VMEM((2, NZ, 8, CX), F32),
            pltpu.VMEM((2, 2, NZ, 8, CX), F32),
            pltpu.VMEM((3, TILES, ANG), F32),
            pltpu.VMEM((3, STEPS * CX, SRCS), BF16),
            pltpu.VMEM((PB, CY, CX), F32),
            pltpu.VMEM((2, PB, CY, CX), F32),
            pltpu.VMEM((2 * STEPS, TILES, CX), F32),
            pltpu.VMEM((2 * outer, inner, 2 * ANG), F32),
            pltpu.VMEM((inner, inner, 2 * ANG), F32),
            dma((8,)),
            dma((NG, 3)),
            dma((STEPS, NG, 4)),
            dma((STEPS, NG, 4)),
            dma((4, 2)),
            dma((4, 2)),
            dma((outer - 1,)),
            dma((outer - 1,)),
            dma((inner - 1,)),
            dma((inner - 1,)),
        ],
        compiler_params=pltpu.CompilerParams(
            collective_id=0, has_side_effects=True, vmem_limit_bytes=56 * 1024 * 1024
        ),
    )(
        *fields,
        rows,
        rows.reshape(1, TILES),
        tile_owner.reshape(1, TILES),
        src_cell.reshape(1, SRCS),
        src_wave.reshape(STEPS, SRCS),
        high,
        low,
        *edge_weights(),
    )


def solution(mesh):
    field = P(None, "gy", "gx")
    return jax.shard_map(
        functools.partial(local, mesh.shape["gx"], mesh.shape["gy"]),
        mesh=mesh,
        in_specs=(field,) * 8
        + (
            P("gy", "gx", None),
            P("gy", "gx", None, None),
            P("gy", "gx", None),
            P("gy", "gx", None, None),
        ),
        out_specs=(field,) * 6 + (P(None, ("gx", "gy")),),
        check_vma=False,
    )
```
